512 devices in a mesh: vol: 8 (over z), row: 8 (over y_lo, core), col: 8 (over x, y_hi).
Axes of the slice: x: 4, y: 8 (y_hi: 2, y_lo: 4; y = y_hi * 4 + y_lo), z: 8, core: 2. Of those that a mesh axis runs over, the one named last changes fastest.
Arguments:
- vol_rhs: bfloat16 [64, 786432], P(None, ('vol', 'row', 'col')), may hold values from -6 to 6
- surf_rhs: bfloat16 [64, 65536], P(None, ('vol', 'row', 'col')), may hold values from -6 to 6
- vol_blocks: bfloat16 [6144, 7, 128, 128], P(('vol', 'row', 'col')), may hold values from -0.1875 to 0.1875
- vol_cols: int32 [6144, 7], P(('vol', 'row', 'col')), may hold values from 0 to 11, as said below
- coupling: bfloat16 [2048, 128, 128], P(('vol', 'row', 'col')), may hold values from -0.5 to 0.5
- trace_map: int32 [2048], P(('vol', 'row', 'col')), may hold values from 0 to 7
- bnd_count: int32 [512], P(('vol', 'row', 'col')), may hold values from 1 to 4
- surf_inverse: bfloat16 [512, 128, 128], P(('vol', 'row', 'col')), may hold values from -0.5 to 0.5
- near_blocks: bfloat16 [512, 8, 4, 128, 128], P(('vol', 'row'), 'col'), may hold values from -0.09375 to 0.09375
- near_cols: int32 [512, 8, 4], P(('vol', 'row'), 'col'), may hold values from 0 to 63
- far_u: bfloat16 [8, 32, 65536], P('col', None, ('vol', 'row')), may hold values from -1 to 1
- far_v: bfloat16 [64, 8, 32, 8192], P(('vol', 'row'), 'col'), may hold values from -0.0625 to 0.0625
Outputs:
- vol_field: float32 [64, 786432], P(None, ('vol', 'row', 'col'))
- surf_field: float32 [64, 65536], P(None, ('vol', 'row', 'col'))
The draws below stay inside these ranges and needn't reach their ends.
Inputs may be any that keep to these rules, and one draw needn't show every extreme that they name: `vol_cols`: row b names 7 different blocks of its own subdomain, the first being b mod 12.
All inputs are finite; a program needn't handle non-finite values.
Results may differ from the reference program's by a relative error of at most 0.01.
Values may be sent and summed in bfloat16 or wider, within the bound.
A program may use at most 64 MiB of HBM per device.

```python
import jax
import jax.numpy as jnp
from jax import lax

ANG = 64
VBLK = 12
SBLK = 1
BS = 128
NNZV = 7
NBND = 4
NEAR = 4
RANK = 32
ITERS = 2
VOLUME = 786432
SURFACE = 65536
VOL_BLOCKS = 6144
SURF_BLOCKS = 512
BND_SLOTS = 2048
GROUP_ROWS = 8192
N_VOL = 8
N_ROW = 8
N_COL = 8
DEVICES = 512


def draw_vol_cols(key, part):
    row_keys = jax.random.split(key, VOL_BLOCKS)

    def offsets_of(row_key):
        return jax.random.permutation(row_key, VBLK - 1)[:NNZV - 1].astype(jnp.int32) + 1
    offsets = jax.vmap(offsets_of)(row_keys)
    own_block = jnp.arange(VOL_BLOCKS, dtype=jnp.int32) % VBLK
    leading = jnp.zeros((VOL_BLOCKS, 1), jnp.int32)
    shifts = jnp.concatenate([leading, offsets], axis=1)
    return ((own_block[:, None] + shifts) % VBLK).astype(jnp.int32)


def touch_ends(entries, rng, low, high):
    place = [jax.random.randint(jax.random.fold_in(rng, axis), (), 0, length) for axis, length in enumerate(entries.shape)]
    widest = entries.shape.index(max(entries.shape))
    beside = place[:widest] + [(place[widest] + 1) % entries.shape[widest]] + place[widest + 1:]
    return entries.at[tuple(place)].set(low).at[tuple(beside)].set(high)


def levels(key, extent, cuts, least, largest):
    level, own = 1.0, jax.random.fold_in(key, 6)
    for position, parts in cuts:
        steps = jnp.exp(jax.random.uniform(jax.random.fold_in(own, position), (parts,), jnp.float32, least / len(cuts), largest / len(cuts)))
        level = level * jnp.repeat(steps, extent[position] // parts).reshape([-1 if axis == position else 1 for axis in range(len(extent))])
    return level


def bell_draw(key, extent, deviation, reach, cuts=(), held_as=jnp.bfloat16):
    entries = deviation * jax.random.normal(key, extent, jnp.float32)
    if cuts:
        entries = entries * levels(key, extent, cuts, -0.22, 0.18)
    return jnp.clip(entries, -reach, reach).astype(held_as)


def setup_inputs(seed: int = 0) -> dict:
    seeds = jax.random.split(jax.random.key(seed), 13)
    return {
        "vol_rhs": bell_draw(seeds[0], (ANG, VOLUME), 1.0, 6.0, ((1, 512),)),
        "surf_rhs": bell_draw(seeds[1], (ANG, SURFACE), 1.0, 6.0, ((1, 512),)),
        "vol_blocks": bell_draw(seeds[2], (VOL_BLOCKS, NNZV, BS, BS), (NNZV * BS) ** -0.5, 0.1875, ((0, 512),)),
        "vol_cols": draw_vol_cols(jax.random.fold_in(seeds[12], 71), 0),
        "coupling": bell_draw(seeds[4], (BND_SLOTS, BS, BS), BS ** -0.5, 0.5, ((0, 512),)),
        "trace_map": touch_ends(jax.random.randint(seeds[5], (BND_SLOTS,), 0, N_VOL * SBLK), jax.random.fold_in(seeds[5], 1), 0, (N_VOL * SBLK) - 1).astype(jnp.int32),
        "bnd_count": touch_ends(jax.random.randint(seeds[6], (DEVICES,), 1, NBND + 1), jax.random.fold_in(seeds[6], 1), 1, NBND).astype(jnp.int32),
        "surf_inverse": bell_draw(seeds[7], (SURF_BLOCKS, BS, BS), BS ** -0.5, 0.5, ((0, 512),)),
        "near_blocks": bell_draw(seeds[8], (SURF_BLOCKS, N_COL, NEAR, BS, BS), (N_COL * NEAR * BS) ** -0.5, 0.09375, ((0, 64), (1, 8))),
        "near_cols": touch_ends(jax.random.randint(seeds[9], (SURF_BLOCKS, N_COL, NEAR), 0, N_VOL * N_ROW * SBLK), jax.random.fold_in(seeds[9], 1), 0, (N_VOL * N_ROW * SBLK) - 1).astype(jnp.int32),
        "far_u": bell_draw(seeds[10], (N_COL, RANK, SURFACE), RANK ** -0.5, 1.0, ((0, 8), (2, 64))),
        "far_v": bell_draw(seeds[11], (N_VOL * N_ROW, N_COL, RANK, GROUP_ROWS), GROUP_ROWS ** -0.5, 0.0625, ((0, 64), (1, 8))),
    }


def halved(value):
    return lax.optimization_barrier(value.astype(jnp.bfloat16))


def volume_solve(field, sub_blocks, sub_columns):
    def subdomain_solve(member):
        local_field, blocks, columns = member
        picked = jnp.take(local_field, columns, axis=1)
        return jnp.einsum("abnk,bnik->abi", picked.astype(jnp.float32), blocks.astype(jnp.float32))

    result = lax.map(subdomain_solve, (jnp.transpose(field, (1, 0, 2, 3)), sub_blocks, sub_columns))
    return jnp.transpose(result, (1, 0, 2, 3))


def reference(vol_rhs, surf_rhs, vol_blocks, vol_cols, coupling, trace_map, bnd_count, surf_inverse, near_blocks, near_cols, far_u, far_v):
    devices = N_VOL * N_ROW * N_COL
    groups = N_ROW * N_COL
    row_groups = N_VOL * N_ROW
    piece_rows = SBLK * BS
    block_slots = N_VOL * SBLK
    sub_blocks = vol_blocks.reshape(devices, VBLK, NNZV, BS, BS)
    sub_columns = vol_cols.reshape(devices, VBLK, NNZV)
    couple = coupling.reshape(devices, NBND, BS, BS).astype(jnp.float32)
    slot_maps = trace_map.reshape(devices, NBND)
    slot_alive = (jnp.arange(NBND, dtype=jnp.int32)[None, :] < bnd_count[:, None]).astype(jnp.float32)
    selector = (slot_maps[:, :, None] == jnp.arange(block_slots, dtype=jnp.int32)[None, None, :]).astype(jnp.float32)
    selector = selector.reshape(N_VOL, groups, NBND, block_slots)
    inverse = surf_inverse.reshape(devices, SBLK, BS, BS).astype(jnp.float32)
    rhs_vol = vol_rhs.astype(jnp.float32).reshape(ANG, devices, VBLK, BS)
    rhs_surf = surf_rhs.astype(jnp.float32)
    near_all = near_blocks.reshape(row_groups, N_COL * SBLK, N_COL, NEAR, BS, BS)
    near_ids = near_cols.reshape(row_groups, N_COL * SBLK, N_COL, NEAR)
    u_parts = jnp.transpose(far_u.reshape(N_COL, RANK, row_groups, N_COL * piece_rows), (2, 0, 1, 3))
    group_of = jnp.arange(devices, dtype=jnp.int32) % groups
    col_index = jnp.arange(N_COL, dtype=jnp.int32)[None, :, None]

    def surface_solve(field):
        blocks = field.astype(jnp.float32).reshape(ANG, devices, SBLK, BS)
        return jnp.einsum("adbk,dbik->adbi", blocks, inverse).reshape(ANG, devices * piece_rows)

    volume = volume_solve(vol_rhs.reshape(ANG, devices, VBLK, BS), sub_blocks, sub_columns)
    surface = surface_solve(surf_rhs)
    for iteration in range(ITERS):
        x_half = halved(volume)
        s_half = halved(surface)
        grouped = jnp.transpose(s_half.reshape(ANG, N_VOL, groups, SBLK, BS), (2, 0, 1, 3, 4)).reshape(groups, ANG, block_slots, BS)
        picked = grouped[group_of[:, None], :, slot_maps, :]
        current = jnp.einsum("djak,djik->adji", picked.astype(jnp.float32), couple) * slot_alive[None, :, :, None]
        padding = jnp.zeros((ANG, devices, VBLK - NBND, BS), jnp.float32)
        resid_vol = halved(rhs_vol - jnp.concatenate([current, padding], axis=2))
        boundary = x_half[:, :, :NBND, :].astype(jnp.float32)
        contrib = jnp.einsum("adji,djik->adjk", boundary, couple) * slot_alive[None, :, :, None]
        traced = jnp.einsum("avgjk,vgjm->agmk", contrib.reshape(ANG, N_VOL, groups, NBND, BS), selector)
        traced = jnp.transpose(traced.reshape(ANG, groups, N_VOL, SBLK, BS), (0, 2, 1, 3, 4)).reshape(ANG, devices * piece_rows)
        column_half = jnp.transpose(s_half.reshape(ANG, row_groups, N_COL, piece_rows), (2, 0, 1, 3)).reshape(N_COL, ANG, row_groups * piece_rows)
        column_wide = column_half.astype(jnp.float32)
        column_blocks = column_half.reshape(N_COL, ANG, row_groups * SBLK, BS)

        def group_rows(member):
            blocks, indices, v_factor, u_factor = member
            gathered = column_blocks[col_index, :, indices, :]
            near_term = jnp.einsum("bcnak,bcnik->abi", gathered.astype(jnp.float32), blocks.astype(jnp.float32))
            coeffs = jnp.einsum("cak,cqk->caq", column_wide, v_factor.astype(jnp.float32))
            coeffs = halved(coeffs).astype(jnp.float32)
            far_term = jnp.einsum("caq,cqi->ai", coeffs, u_factor.astype(jnp.float32))
            return near_term.reshape(ANG, N_COL * piece_rows) + far_term

        integral = lax.map(group_rows, (near_all, near_ids, far_v, u_parts))
        integral = jnp.transpose(integral, (1, 0, 2)).reshape(ANG, devices * piece_rows)
        resid_surf = halved(rhs_surf - integral - traced)
        volume = volume_solve(resid_vol, sub_blocks, sub_columns)
        surface = surface + surface_solve(resid_surf)
    return volume.reshape(ANG, devices * VBLK * BS), surface
```

```python
import functools

import jax
import jax.numpy as jnp
from jax import lax
from jax.experimental import pallas as pl
from jax.experimental.pallas import tpu as pltpu
from jax.sharding import PartitionSpec as P

BS = 128
ITERS = 2
CORES = 2
Y_HALVES = 2
MESH = pl.DeviceIdType.MESH
F32 = jnp.float32
BF16 = jnp.bfloat16


def dot_nt(a, b):
    return lax.dot_general(a, b, (((1,), (1,)), ((), ())), preferred_element_type=F32)


def dot_nn(a, b):
    return lax.dot_general(a, b, (((1,), (0,)), ((), ())), preferred_element_type=F32)


def kernel(
    sizes,
    vol_cols,
    trace_map,
    bnd_count,
    near_cols,
    vol_rhs,
    surf_rhs,
    vol_blocks,
    coupling,
    surf_inverse,
    near_blocks,
    far_u,
    far_v,
    vol_out,
    surf_out,
    rhs4,
    field,
    rhs_surf,
    blocks,
    couple,
    inverse,
    near,
    u_mat,
    v_mat,
    gat_a0,
    gat_b0,
    gat_a1,
    gat_b1,
    tr_send,
    tr_recv,
    row_send,
    row_recv,
    row_own,
    surface,
    vol_res,
    load_sem,
    store_sem,
    a1_send,
    a1_recv,
    b1_send,
    b1_recv,
    a2_send,
    a2_recv,
    b2_send,
    b2_recv,
    ca_send,
    ca_recv,
    cb_send,
    cb_recv,
    tr_ssem,
    tr_rsem,
    row_ssem,
    row_rsem,
):
    gat_a, gat_b = (gat_a0, gat_a1), (gat_b0, gat_b1)
    nz, ny, nx = sizes
    ncol = nx * Y_HALVES
    angles = rhs_surf.shape[0]
    half = angles // 2
    nblk = field.shape[0]
    nnz = blocks.shape[1]
    slots = couple.shape[0]
    nears = near.shape[1]

    z = lax.axis_index("vol")
    row = lax.axis_index("row")
    col = lax.axis_index("col")
    y, core = row // CORES, row % CORES
    x, y_hi = col // Y_HALVES, col % Y_HALVES

    def z_peer(o):
        return lax.rem(z + o, nz)

    def y_peer(o):
        return lax.rem(y + o, ny)

    def col_peer(o):
        return lax.rem(x + o // Y_HALVES, nx) * Y_HALVES + lax.rem(y_hi + o % Y_HALVES, Y_HALVES)

    partner = y * CORES + (1 - core)

    loads = []

    def load(src, dst):
        copy = pltpu.make_async_copy(src, dst, load_sem.at[len(loads)])
        copy.start()
        loads.append(copy)
        return copy

    ld_rhs_surf = load(surf_rhs, rhs_surf)
    ld_inverse = load(surf_inverse.at[0], inverse)

    barrier = pltpu.get_barrier_semaphore()
    for o in range(1, nz):
        pl.semaphore_signal(barrier, inc=1, device_id={"vol": z_peer(o)}, device_id_type=MESH)
    for o in range(1, ny):
        pl.semaphore_signal(
            barrier, inc=1, device_id={"row": y_peer(o) * CORES + core}, device_id_type=MESH
        )
    pl.semaphore_signal(barrier, inc=1, device_id={"row": partner}, device_id_type=MESH)
    for o in range(1, ncol):
        pl.semaphore_signal(barrier, inc=1, device_id={"col": col_peer(o)}, device_id_type=MESH)

    ld_field = [load(vol_rhs.at[:, b * BS : (b + 1) * BS], field.at[b]) for b in range(nblk)]
    ld_rhs4 = [load(vol_rhs.at[:, b * BS : (b + 1) * BS], rhs4.at[b]) for b in range(slots)]
    ld_blocks = load(vol_blocks.at[0:slots], blocks.at[0:slots])
    ld_couple = load(coupling, couple)
    ld_v = load(far_v.at[0, 0], v_mat)
    ld_u = load(far_u.at[0], u_mat)
    ld_near = load(near_blocks.at[:, 0], near)
    ld_rest = load(vol_blocks.at[slots:nblk], blocks.at[slots:nblk])

    ld_rhs_surf.wait()
    ld_inverse.wait()
    surface[...] = dot_nt(rhs_surf[...], inverse[...])

    sends = []

    def send(src, dst, ssem, rsem, device):
        copy = pltpu.make_async_remote_copy(
            src_ref=src, dst_ref=dst, send_sem=ssem, recv_sem=rsem, device_id=device,
            device_id_type=MESH,
        )
        copy.start()
        sends.append(copy)

    def arrived(dst, rsem, ssem):
        pltpu.make_async_remote_copy(
            src_ref=dst, dst_ref=dst, send_sem=ssem, recv_sem=rsem,
            device_id={"row": partner}, device_id_type=MESH,
        ).wait_recv()

    def gather_start(it):
        s_half = surface[...].astype(BF16)
        gat_a[it][core, y, z] = s_half[0:half]
        gat_b[it][core, z, y] = s_half[half:angles]
        if it == 0:
            pl.semaphore_wait(barrier, (nz - 1) + (ny - 1) + 1 + (ncol - 1))
        own_a = gat_a[it].at[core, y, z]
        own_b = gat_b[it].at[core, z, y]
        for o in [k for d in range(nz // 2, 0, -1) for k in sorted({d, nz - d})]:
            send(own_a, own_a, a1_send.at[it, o], a1_recv.at[it, z], {"vol": z_peer(o)})
        for o in range(1, ny):
            dev = {"row": y_peer(o) * CORES + core}
            send(own_b, own_b, b1_send.at[it, o], b1_recv.at[it, y], dev)

    def gather_finish(it):
        for o in range(1, ny):
            src = y_peer(o)
            arrived(gat_b[it].at[core, z, src], b1_recv.at[it, src], b1_send.at[it, o])
        mine_b = gat_b[it].at[core, z]
        for o in [k for d in range(nz // 2, 0, -1) for k in sorted({d, nz - d})]:
            send(mine_b, mine_b, b2_send.at[it, o], b2_recv.at[it, z], {"vol": z_peer(o)})
        send(mine_b, mine_b, cb_send.at[it, 0], cb_recv.at[it, z], {"row": partner})
        for o in range(1, nz):
            src = z_peer(o)
            arrived(gat_a[it].at[core, y, src], a1_recv.at[it, src], a1_send.at[it, o])
        mine_a = gat_a[it].at[core, y]
        for o in range(1, ny):
            dev = {"row": y_peer(o) * CORES + core}
            send(mine_a, mine_a, a2_send.at[it, o], a2_recv.at[it, y], dev)
        send(mine_a, mine_a, ca_send.at[it, 0], ca_recv.at[it, y], {"row": partner})
        for o in [k for d in range(1, nz // 2 + 1) for k in sorted({d, nz - d})]:
            src = z_peer(o)
            ref = gat_b[it].at[core, src]
            arrived(ref, b2_recv.at[it, src], b2_send.at[it, o])
            send(ref, ref, cb_send.at[it, o], cb_recv.at[it, src], {"row": partner})
        for o in range(1, ny):
            src = y_peer(o)
            ref = gat_a[it].at[core, src]
            arrived(ref, a2_recv.at[it, src], a2_send.at[it, o])
            send(ref, ref, ca_send.at[it, o], ca_recv.at[it, src], {"row": partner})
        for o in range(nz):
            src = z_peer(o)
            arrived(gat_b[it].at[1 - core, src], cb_recv.at[it, src], cb_send.at[it, o])
        for o in range(ny):
            src = y_peer(o)
            arrived(gat_a[it].at[1 - core, src], ca_recv.at[it, src], ca_send.at[it, o])

    def piece(it, k, j, v):
        return jnp.concatenate([gat_a[it][k, j, v], gat_b[it][k, v, j]], axis=0)

    def volume_block(b):
        total = dot_nt(field[vol_cols[b, 0]], blocks[b, 0])
        for n in range(1, nnz):
            total += dot_nt(field[vol_cols[b, n]], blocks[b, n])
        return total

    def alive(j):
        return jnp.where(j < bnd_count[0], 1.0, 0.0).astype(F32)

    def traces(it):
        parts = []
        for j in range(slots):
            x_half = volume_block(j).astype(BF16)
            parts.append(dot_nn(x_half, couple[j]) * alive(j))
        for m in range(nz):
            total = None
            for j in range(slots):
                term = parts[j] * jnp.where(trace_map[j] == m, 1.0, 0.0).astype(F32)
                total = term if total is None else total + term
            tr_send[it, m] = total.astype(BF16)

    def traces_send(it):
        for o in [k for d in range(nz // 2, 0, -1) for k in sorted({d, nz - d})]:
            dst = z_peer(o)
            send(
                tr_send.at[it, dst], tr_recv.at[it, z], tr_ssem.at[it, o], tr_rsem.at[it, z],
                {"vol": dst},
            )

    def coeffs_of(it):
        def step(index, total):
            v, j = index // ny, index % ny
            for k in range(CORES):
                start = pl.multiple_of((v * ny * CORES + j * CORES + k) * BS, BS)
                total += dot_nt(piece(it, k, j, v), v_mat[:, pl.ds(start, BS)])
            return total

        zero = jnp.zeros((angles, v_mat.shape[0]), F32)
        return lax.fori_loop(0, nz * ny, step, zero, unroll=8)

    def integral_block(it, coeffs, b):
        start = pl.multiple_of(b * BS, BS)
        total = dot_nn(coeffs, u_mat[:, pl.ds(start, BS)])
        for n in range(nears):
            index = near_cols[b, n]
            v, rest = index // (ny * CORES), index % (ny * CORES)
            total += dot_nt(piece(it, rest % CORES, rest // CORES, v), near[b, n])
        return total

    def integral_send(it, coeffs):
        for o in [ncol - 1 - k for k in range(ncol - 1)]:
            dst = col_peer(o)
            row_send[it, dst] = integral_block(it, coeffs, dst).astype(BF16)
            send(
                row_send.at[it, dst], row_recv.at[it, col], row_ssem.at[it, o],
                row_rsem.at[it, col], {"col": dst},
            )
        row_own[...] = integral_block(it, coeffs, col)

    def residual(it):
        for j in range(slots):
            index = trace_map[j]
            current = dot_nt(piece(it, core, y, index), couple[j]) * alive(j)
            field[j] = (rhs4[j].astype(F32) - current).astype(BF16)

    def surface_step(it):
        total = row_own[...] + tr_send[it, z].astype(F32)
        for o in range(1, nz):
            src = z_peer(o)
            arrived(tr_recv.at[it, src], tr_rsem.at[it, src], tr_ssem.at[it, o])
            total += tr_recv[it, src].astype(F32)
        for o in range(1, ncol):
            src = col_peer(o)
            arrived(row_recv.at[it, src], row_rsem.at[it, src], row_ssem.at[it, o])
            total += row_recv[it, src].astype(F32)
        resid = (rhs_surf[...].astype(F32) - total).astype(BF16)
        surface[...] += dot_nt(resid, inverse[...])

    stores = []
    for it in range(ITERS):
        gather_start(it)
        if it == 0:
            for copy in ld_field + ld_rhs4:
                copy.wait()
            ld_blocks.wait()
            ld_couple.wait()
            traces(0)
        gather_finish(it)
        if it == 0:
            ld_v.wait()
            ld_u.wait()
            ld_near.wait()
        coeffs = coeffs_of(it).astype(BF16)
        integral_send(it, coeffs)
        traces_send(it)
        residual(it)
        if it + 1 < ITERS:
            traces(it + 1)
        else:
            ld_rest.wait()
            for b in range(nblk):
                vol_res[b] = volume_block(b)
                copy = pltpu.make_async_copy(
                    vol_res.at[b], vol_out.at[:, b * BS : (b + 1) * BS], store_sem.at[b]
                )
                copy.start()
                stores.append(copy)
        surface_step(it)
    copy = pltpu.make_async_copy(surface, surf_out, store_sem.at[nblk])
    copy.start()
    stores.append(copy)
    for copy in sends:
        copy.wait_send()
    for copy in stores:
        copy.wait()


def local(
    sizes,
    vol_rhs,
    surf_rhs,
    vol_blocks,
    vol_cols,
    coupling,
    trace_map,
    bnd_count,
    surf_inverse,
    near_blocks,
    near_cols,
    far_u,
    far_v,
):
    nz, ny, nx = sizes
    ncol = nx * Y_HALVES
    angles = vol_rhs.shape[0]
    half = angles // 2
    nblk, nnz = vol_cols.shape
    slots = coupling.shape[0]
    rank = far_u.shape[1]
    nears = near_blocks.shape[2]
    smem = pl.BlockSpec(memory_space=pltpu.SMEM)
    hbm = pl.BlockSpec(memory_space=pl.ANY)
    dma = pltpu.SemaphoreType.DMA
    return pl.pallas_call(
        functools.partial(kernel, sizes),
        out_shape=(
            jax.ShapeDtypeStruct((angles, nblk * BS), F32),
            jax.ShapeDtypeStruct((angles, BS), F32),
        ),
        in_specs=[smem] * 4 + [hbm] * 8,
        out_specs=(hbm, hbm),
        scratch_shapes=[
            pltpu.VMEM((slots, angles, BS), BF16),
            pltpu.VMEM((nblk, angles, BS), BF16),
            pltpu.VMEM((angles, BS), BF16),
            pltpu.VMEM((nblk, nnz, BS, BS), BF16),
            pltpu.VMEM((slots, BS, BS), BF16),
            pltpu.VMEM((BS, BS), BF16),
            pltpu.VMEM((ncol, nears, BS, BS), BF16),
            pltpu.VMEM((rank, ncol * BS), BF16),
            pltpu.VMEM((rank, nz * ny * CORES * BS), BF16),
            pltpu.VMEM((CORES, ny, nz, half, BS), BF16),
            pltpu.VMEM((CORES, nz, ny, half, BS), BF16),
            pltpu.VMEM((CORES, ny, nz, half, BS), BF16),
            pltpu.VMEM((CORES, nz, ny, half, BS), BF16),
            pltpu.VMEM((ITERS, nz, angles, BS), BF16),
            pltpu.VMEM((ITERS, nz, angles, BS), BF16),
            pltpu.VMEM((ITERS, ncol, angles, BS), BF16),
            pltpu.VMEM((ITERS, ncol, angles, BS), BF16),
            pltpu.VMEM((angles, BS), F32),
            pltpu.VMEM((angles, BS), F32),
            pltpu.VMEM((nblk, angles, BS), F32),
            dma((nblk + slots + 8,)),
            dma((nblk + 1,)),
            dma((ITERS, nz)),
            dma((ITERS, nz)),
            dma((ITERS, ny)),
            dma((ITERS, ny)),
            dma((ITERS, ny)),
            dma((ITERS, ny)),
            dma((ITERS, nz)),
            dma((ITERS, nz)),
            dma((ITERS, ny)),
            dma((ITERS, ny)),
            dma((ITERS, nz)),
            dma((ITERS, nz)),
            dma((ITERS, nz)),
            dma((ITERS, nz)),
            dma((ITERS, ncol)),
            dma((ITERS, ncol)),
        ],
        compiler_params=pltpu.CompilerParams(
            collective_id=0, has_side_effects=True, vmem_limit_bytes=60 * 2**20
        ),
    )(
        vol_cols,
        trace_map,
        bnd_count,
        near_cols[:, 0],
        vol_rhs,
        surf_rhs,
        vol_blocks,
        coupling,
        surf_inverse,
        near_blocks,
        far_u,
        far_v,
    )


def solution(mesh):
    sizes = (mesh.shape["vol"], mesh.shape["row"] // CORES, mesh.shape["col"] // Y_HALVES)
    everywhere = ("vol", "row", "col")
    in_specs = (
        P(None, everywhere),
        P(None, everywhere),
        P(everywhere, None, None, None),
        P(everywhere, None),
        P(everywhere, None, None),
        P(everywhere),
        P(everywhere),
        P(everywhere, None, None),
        P(("vol", "row"), "col", None, None, None),
        P(("vol", "row"), "col", None),
        P("col", None, ("vol", "row")),
        P(("vol", "row"), "col", None, None),
    )
    out_specs = (P(None, everywhere), P(None, everywhere))
    return jax.shard_map(
        functools.partial(local, sizes), mesh=mesh, in_specs=in_specs, out_specs=out_specs,
        check_vma=False,
    )
```

```python
import functools

import jax
import jax.numpy as jnp
from jax import lax
from jax.experimental import pallas as pl
from jax.experimental.pallas import tpu as pltpu
from jax.sharding import PartitionSpec as P

BS = 128
ITERS = 2
CORES = 2
Y_HALVES = 2
MESH = pl.DeviceIdType.MESH
F32 = jnp.float32
BF16 = jnp.bfloat16


def dot_nt(a, b):
    return lax.dot_general(a, b, (((1,), (1,)), ((), ())), preferred_element_type=F32)


def dot_nn(a, b):
    return lax.dot_general(a, b, (((1,), (0,)), ((), ())), preferred_element_type=F32)


def kernel(
    sizes,
    vol_cols_hbm,
    trace_map_hbm,
    bnd_count_hbm,
    near_cols_hbm,
    vol_rhs,
    surf_rhs,
    vol_blocks,
    coupling,
    surf_inverse,
    near_blocks,
    far_u,
    far_v,
    vol_out,
    surf_out,
    vol_cols,
    trace_map,
    bnd_count,
    near_cols,
    rhs4,
    field,
    rhs_surf,
    blocks,
    couple,
    inverse,
    near,
    u_mat,
    v_mat,
    gat0,
    gat1,
    tr_send,
    tr_recv,
    row_send,
    row_recv,
    row_own,
    surface,
    load_sem,
    zo_send,
    zo_recv,
    yo_send,
    yo_recv,
    af_send,
    af_recv,
    bf_send,
    bf_recv,
    co_send,
    co_recv,
    tr_ssem,
    tr_rsem,
    row_ssem,
    row_rsem,
):
    gat = (gat0, gat1)
    nz, ny, nx = sizes
    ncol = nx * Y_HALVES
    angles = rhs_surf.shape[0]
    half = angles // 2
    nblk = field.shape[0]
    nnz = blocks.shape[1]
    slots = couple.shape[0]
    nears = near.shape[1]

    z = lax.axis_index("vol")
    row = lax.axis_index("row")
    col = lax.axis_index("col")
    y, core = row // CORES, row % CORES
    x, y_hi = col // Y_HALVES, col % Y_HALVES

    def z_peer(o):
        return lax.rem(z + o, nz)

    def y_peer(o):
        return lax.rem(y + o, ny)

    def col_peer(o):
        return lax.rem(x + o // Y_HALVES, nx) * Y_HALVES + lax.rem(y_hi + o % Y_HALVES, Y_HALVES)

    partner = y * CORES + (1 - core)

    loads = []

    def load(src, dst):
        copy = pltpu.make_async_copy(src, dst, load_sem.at[len(loads)])
        copy.start()
        loads.append(copy)
        return copy

    ld_rhs_surf = load(surf_rhs, rhs_surf)
    ld_inverse = load(surf_inverse.at[0], inverse)

    barrier = pltpu.get_barrier_semaphore()
    for o in range(1, nz):
        pl.semaphore_signal(barrier, inc=1, device_id={"vol": z_peer(o)}, device_id_type=MESH)
    for o in range(1, ny):
        pl.semaphore_signal(
            barrier, inc=1, device_id={"row": y_peer(o) * CORES + core}, device_id_type=MESH
        )
    pl.semaphore_signal(barrier, inc=1, device_id={"row": partner}, device_id_type=MESH)
    for o in range(1, ncol):
        pl.semaphore_signal(barrier, inc=1, device_id={"col": col_peer(o)}, device_id_type=MESH)

    ld_tables = [
        load(vol_cols_hbm, vol_cols),
        load(trace_map_hbm, trace_map),
        load(bnd_count_hbm, bnd_count),
        load(near_cols_hbm, near_cols),
    ]
    ld_field = [load(vol_rhs.at[:, b * BS : (b + 1) * BS], field.at[b]) for b in range(nblk)]
    ld_rhs4 = [load(vol_rhs.at[:, b * BS : (b + 1) * BS], rhs4.at[b]) for b in range(slots)]
    ld_blocks = load(vol_blocks.at[0:slots], blocks.at[0:slots])
    ld_couple = load(coupling, couple)
    ld_v = load(far_v.at[0, 0], v_mat)
    ld_u = load(far_u.at[0], u_mat)
    ld_near = load(near_blocks.at[:, 0], near)
    ld_rest = load(vol_blocks.at[slots:nblk], blocks.at[slots:nblk])

    ld_rhs_surf.wait()
    ld_inverse.wait()
    surface[...] = dot_nt(rhs_surf[...], inverse[...])

    sends = []

    def send(src, dst, ssem, rsem, device):
        copy = pltpu.make_async_remote_copy(
            src_ref=src, dst_ref=dst, send_sem=ssem, recv_sem=rsem, device_id=device,
            device_id_type=MESH,
        )
        copy.start()
        sends.append(copy)

    def arrived(dst, rsem, ssem):
        pltpu.make_async_remote_copy(
            src_ref=dst, dst_ref=dst, send_sem=ssem, recv_sem=rsem,
            device_id={"row": partner}, device_id_type=MESH,
        ).wait_recv()

    z_far_first = [k for d in range(nz // 2, 0, -1) for k in sorted({d, nz - d})]
    z_near_first = z_far_first[::-1]
    y_order = sorted(range(1, ny), key=lambda o: abs(o - ny / 2))

    def gather_start(it):
        own = gat[it].at[core, z, y]
        own[...] = surface[...].astype(BF16)
        if it == 0:
            pl.semaphore_wait(barrier, (nz - 1) + (ny - 1) + 1 + (ncol - 1))
        for o in z_far_first:
            send(own, own, zo_send.at[it, o], zo_recv.at[it, z], {"vol": z_peer(o)})
        for o in y_order:
            dev = {"row": y_peer(o) * CORES + core}
            send(own, own, yo_send.at[it, o], yo_recv.at[it, y], dev)
        send(own, own, co_send.at[it, 0, 0], co_recv.at[it, z, y], {"row": partner})

    def from_z(it, oz):
        src = z_peer(oz)
        ref = gat[it].at[core, src, y]
        arrived(ref, zo_recv.at[it, src], zo_send.at[it, oz])
        first = ref.at[0:half]
        for oy in y_order:
            dev = {"row": y_peer(oy) * CORES + core}
            send(first, first, af_send.at[it, oz, oy], af_recv.at[it, src, y], dev)
        send(ref, ref, co_send.at[it, oz, 0], co_recv.at[it, src, y], {"row": partner})

    def from_y(it, oy):
        src = y_peer(oy)
        ref = gat[it].at[core, z, src]
        arrived(ref, yo_recv.at[it, src], yo_send.at[it, oy])
        second = ref.at[half:angles]
        for oz in z_far_first:
            send(
                second, second, bf_send.at[it, oz, oy], bf_recv.at[it, z, src],
                {"vol": z_peer(oz)},
            )
        send(ref, ref, co_send.at[it, 0, oy], co_recv.at[it, z, src], {"row": partner})

    def from_both(it, oz, oy):
        z_src, y_src = z_peer(oz), y_peer(oy)
        ref = gat[it].at[core, z_src, y_src]
        arrived(ref.at[0:half], af_recv.at[it, z_src, y_src], af_send.at[it, oz, oy])
        arrived(ref.at[half:angles], bf_recv.at[it, z_src, y_src], bf_send.at[it, oz, oy])
        send(ref, ref, co_send.at[it, oz, oy], co_recv.at[it, z_src, y_src], {"row": partner})

    def far_part(it, k, oz):
        v = z_peer(oz)
        lhs, rhs = [], []
        for j in range(ny):
            lhs.append(gat[it][k, v, j])
            start = pl.multiple_of((v * ny * CORES + j * CORES + k) * BS, BS)
            rhs.append(v_mat[:, pl.ds(start, BS)])
        return dot_nt(jnp.concatenate(lhs, axis=1), jnp.concatenate(rhs, axis=1))

    def gather_finish(it):
        legs = [(d, 1, o) for o in z_near_first for d in [2 * min(o, nz - o)]]
        legs += [(3 if o == ny // 2 else 5, 0, o) for o in y_order]
        for _, along_z, o in sorted(legs):
            if along_z:
                from_z(it, o)
            else:
                from_y(it, o)
        for oz in z_near_first:
            for oy in y_order:
                from_both(it, oz, oy)
        if it == 0:
            ld_v.wait()
        total = None
        for oz in [0] + z_near_first:
            term = far_part(it, core, oz)
            total = term if total is None else total + term
        for oz in [0] + z_near_first:
            v = z_peer(oz)
            for oy in [0] + y_order:
                j = y_peer(oy)
                arrived(gat[it].at[1 - core, v, j], co_recv.at[it, v, j], co_send.at[it, oz, oy])
            total += far_part(it, 1 - core, oz)
        return total.astype(BF16)

    def volume_block(b):
        lhs = jnp.concatenate([field[vol_cols[n, b]] for n in range(nnz)], axis=1)
        rhs = jnp.concatenate([blocks[b, n] for n in range(nnz)], axis=1)
        return dot_nt(lhs, rhs)

    def alive(j):
        return jnp.where(j < bnd_count[0], 1.0, 0.0).astype(F32)

    def traces(it):
        parts = []
        for j in range(slots):
            x_half = volume_block(j).astype(BF16)
            parts.append(dot_nn(x_half, couple[j]) * alive(j))
        for m in range(nz):
            total = None
            for j in range(slots):
                term = parts[j] * jnp.where(trace_map[j] == m, 1.0, 0.0).astype(F32)
                total = term if total is None else total + term
            tr_send[it, m] = total.astype(BF16)

    def traces_send(it):
        for o in [k for d in range(nz // 2, 0, -1) for k in sorted({d, nz - d})]:
            dst = z_peer(o)
            send(
                tr_send.at[it, dst], tr_recv.at[it, z], tr_ssem.at[it, o], tr_rsem.at[it, z],
                {"vol": dst},
            )

    def integral_block(it, coeffs, b):
        start = pl.multiple_of(b * BS, BS)
        lhs, rhs = [], []
        for n in range(nears):
            index = near_cols[n, b]
            v, rest = index // (ny * CORES), index % (ny * CORES)
            lhs.append(gat[it][rest % CORES, v, rest // CORES])
            rhs.append(near[b, n])
        total = dot_nt(jnp.concatenate(lhs, axis=1), jnp.concatenate(rhs, axis=1))
        return total + dot_nn(coeffs, u_mat[:, pl.ds(start, BS)])

    col_order = sorted(
        range(1, ncol), key=lambda o: (-(o % Y_HALVES), abs(o // Y_HALVES - nx / 2))
    )

    def integral_send(it, coeffs):
        for o in col_order:
            dst = col_peer(o)
            row_send[it, dst] = integral_block(it, coeffs, dst).astype(BF16)
            send(
                row_send.at[it, dst], row_recv.at[it, col], row_ssem.at[it, o],
                row_rsem.at[it, col], {"col": dst},
            )
        row_own[...] = integral_block(it, coeffs, col)

    def residual(it):
        for j in range(slots):
            index = trace_map[j]
            current = dot_nt(gat[it][core, index, y], couple[j]) * alive(j)
            field[j] = (rhs4[j].astype(F32) - current).astype(BF16)

    def surface_step(it):
        total = row_own[...] + tr_send[it, z].astype(F32)
        for o in range(1, nz):
            src = z_peer(o)
            arrived(tr_recv.at[it, src], tr_rsem.at[it, src], tr_ssem.at[it, o])
            total += tr_recv[it, src].astype(F32)
        for o in range(1, ncol):
            src = col_peer(o)
            arrived(row_recv.at[it, src], row_rsem.at[it, src], row_ssem.at[it, o])
            total += row_recv[it, src].astype(F32)
        resid = (rhs_surf[...].astype(F32) - total).astype(BF16)
        surface[...] += dot_nt(resid, inverse[...])

    for it in range(ITERS):
        if it == 0:
            for copy in ld_tables + ld_field + ld_rhs4:
                copy.wait()
            ld_blocks.wait()
            ld_couple.wait()
            traces(0)
        gather_start(it)
        coeffs = gather_finish(it)
        if it == 0:
            ld_u.wait()
            ld_near.wait()
        integral_send(it, coeffs)
        traces_send(it)
        residual(it)
        if it + 1 < ITERS:
            traces(it + 1)
        else:
            ld_rest.wait()
            for b in range(nblk):
                vol_out[:, b * BS : (b + 1) * BS] = volume_block(b)
        surface_step(it)
    surf_out[...] = surface[...]
    for copy in sends:
        copy.wait_send()


def in_hbm(x):
    if x.size == 1:
        return x
    return pltpu.with_memory_space_constraint(x, pltpu.HBM)


def local(
    sizes,
    vol_rhs,
    surf_rhs,
    vol_blocks,
    vol_cols,
    coupling,
    trace_map,
    bnd_count,
    surf_inverse,
    near_blocks,
    near_cols,
    far_u,
    far_v,
):
    nz, ny, nx = sizes
    ncol = nx * Y_HALVES
    angles = vol_rhs.shape[0]
    nblk, nnz = vol_cols.shape
    slots = coupling.shape[0]
    rank = far_u.shape[1]
    nears = near_blocks.shape[2]
    hbm = pl.BlockSpec(memory_space=pltpu.HBM)
    dma = pltpu.SemaphoreType.DMA
    return pl.pallas_call(
        functools.partial(kernel, sizes),
        out_shape=(
            jax.ShapeDtypeStruct((angles, nblk * BS), F32),
            jax.ShapeDtypeStruct((angles, BS), F32),
        ),
        in_specs=[hbm] * 2 + [pl.BlockSpec(memory_space=pl.ANY)] + [hbm] * 9,
        out_specs=(pl.BlockSpec(memory_space=pltpu.VMEM),) * 2,
        scratch_shapes=[
            pltpu.SMEM((nnz, nblk), jnp.int32),
            pltpu.SMEM((slots,), jnp.int32),
            pltpu.SMEM((1,), jnp.int32),
            pltpu.SMEM((nears, ncol), jnp.int32),
            pltpu.VMEM((slots, angles, BS), BF16),
            pltpu.VMEM((nblk, angles, BS), BF16),
            pltpu.VMEM((angles, BS), BF16),
            pltpu.VMEM((nblk, nnz, BS, BS), BF16),
            pltpu.VMEM((slots, BS, BS), BF16),
            pltpu.VMEM((BS, BS), BF16),
            pltpu.VMEM((ncol, nears, BS, BS), BF16),
            pltpu.VMEM((rank, ncol * BS), BF16),
            pltpu.VMEM((rank, nz * ny * CORES * BS), BF16),
            pltpu.VMEM((CORES, nz, ny, angles, BS), BF16),
            pltpu.VMEM((CORES, nz, ny, angles, BS), BF16),
            pltpu.VMEM((ITERS, nz, angles, BS), BF16),
            pltpu.VMEM((ITERS, nz, angles, BS), BF16),
            pltpu.VMEM((ITERS, ncol, angles, BS), BF16),
            pltpu.VMEM((ITERS, ncol, angles, BS), BF16),
            pltpu.VMEM((angles, BS), F32),
            pltpu.VMEM((angles, BS), F32),
            dma((nblk + slots + 12,)),
            dma((ITERS, nz)),
            dma((ITERS, nz)),
            dma((ITERS, ny)),
            dma((ITERS, ny)),
            dma((ITERS, nz, ny)),
            dma((ITERS, nz, ny)),
            dma((ITERS, nz, ny)),
            dma((ITERS, nz, ny)),
            dma((ITERS, nz, ny)),
            dma((ITERS, nz, ny)),
            dma((ITERS, nz)),
            dma((ITERS, nz)),
            dma((ITERS, ncol)),
            dma((ITERS, ncol)),
        ],
        compiler_params=pltpu.CompilerParams(
            collective_id=0, has_side_effects=True, vmem_limit_bytes=16 * 2**20
        ),
    )(*map(
        in_hbm, (vol_cols.T,
        trace_map,
        bnd_count,
        near_cols[:, 0].T,
        vol_rhs,
        surf_rhs,
        vol_blocks,
        coupling,
        surf_inverse,
        near_blocks,
        far_u,
        far_v,
    )))


def solution(mesh):
    sizes = (mesh.shape["vol"], mesh.shape["row"] // CORES, mesh.shape["col"] // Y_HALVES)
    everywhere = ("vol", "row", "col")
    in_specs = (
        P(None, everywhere),
        P(None, everywhere),
        P(everywhere, None, None, None),
        P(everywhere, None),
        P(everywhere, None, None),
        P(everywhere),
        P(everywhere),
        P(everywhere, None, None),
        P(("vol", "row"), "col", None, None, None),
        P(("vol", "row"), "col", None),
        P("col", None, ("vol", "row")),
        P(("vol", "row"), "col", None, None),
    )
    out_specs = (P(None, everywhere), P(None, everywhere))
    return jax.shard_map(
        functools.partial(local, sizes), mesh=mesh, in_specs=in_specs, out_specs=out_specs,
        check_vma=False,
    )
```

```python
import functools

import jax
import jax.numpy as jnp
from jax import lax
from jax.experimental import pallas as pl
from jax.experimental.pallas import tpu as pltpu
from jax.sharding import PartitionSpec as P

BS = 128
ITERS = 2
CORES = 2
Y_HALVES = 2
MESH = pl.DeviceIdType.MESH
CORNER = {(1, 1): 'AB', (1, 2): 'AB', (2, 1): 'AB', (2, 2): 'AB', (3, 1): 'AB', (3, 2): 'AB', (4, 1): 'AB', (4, 2): 'AB'}
NEAR_FIRST = True
F32 = jnp.float32
BF16 = jnp.bfloat16


def dot_nt(a, b):
    return lax.dot_general(a, b, (((1,), (1,)), ((), ())), preferred_element_type=F32)


def dot_nn(a, b):
    return lax.dot_general(a, b, (((1,), (0,)), ((), ())), preferred_element_type=F32)


def kernel(
    sizes,
    vol_cols_hbm,
    trace_map_hbm,
    bnd_count_hbm,
    near_cols_hbm,
    vol_rhs,
    surf_rhs,
    vol_blocks,
    coupling,
    surf_inverse,
    near_blocks,
    far_u,
    far_v,
    vol_out,
    surf_out,
    vol_cols,
    trace_map,
    bnd_count,
    near_cols,
    rhs4,
    field,
    rhs_surf,
    blocks,
    couple,
    inverse,
    near,
    u_mat,
    v_mat,
    gat0,
    gat1,
    tr_send,
    tr_recv,
    row_send,
    row_recv,
    row_own,
    surface,
    load_sem,
    zo_send,
    zo_recv,
    yo_send,
    yo_recv,
    af_send,
    af_recv,
    bf_send,
    bf_recv,
    co_send,
    co_recv,
    tr_ssem,
    tr_rsem,
    row_ssem,
    row_rsem,
):
    gat = (gat0, gat1)
    nz, ny, nx = sizes
    ncol = nx * Y_HALVES
    angles = rhs_surf.shape[0]
    half = angles // 2
    nblk = field.shape[0]
    nnz = blocks.shape[1]
    slots = couple.shape[0]
    nears = near.shape[1]

    z = lax.axis_index("vol")
    row = lax.axis_index("row")
    col = lax.axis_index("col")
    y, core = row // CORES, row % CORES
    x, y_hi = col // Y_HALVES, col % Y_HALVES

    def z_peer(o):
        return lax.rem(z + o, nz)

    def y_peer(o):
        return lax.rem(y + o, ny)

    def col_peer(o):
        return lax.rem(x + o // Y_HALVES, nx) * Y_HALVES + lax.rem(y_hi + o % Y_HALVES, Y_HALVES)

    partner = y * CORES + (1 - core)

    loads = []

    def load(src, dst):
        copy = pltpu.make_async_copy(src, dst, load_sem.at[len(loads)])
        copy.start()
        loads.append(copy)
        return copy

    ld_rhs_surf = load(surf_rhs, rhs_surf)
    ld_inverse = load(surf_inverse.at[0], inverse)

    barrier = pltpu.get_barrier_semaphore()
    for o in range(1, nz):
        pl.semaphore_signal(barrier, inc=1, device_id={"vol": z_peer(o)}, device_id_type=MESH)
    for o in range(1, ny):
        pl.semaphore_signal(
            barrier, inc=1, device_id={"row": y_peer(o) * CORES + core}, device_id_type=MESH
        )
    pl.semaphore_signal(barrier, inc=1, device_id={"row": partner}, device_id_type=MESH)
    for o in range(1, ncol):
        pl.semaphore_signal(barrier, inc=1, device_id={"col": col_peer(o)}, device_id_type=MESH)

    ld_tables = [
        load(vol_cols_hbm, vol_cols),
        load(trace_map_hbm, trace_map),
        load(bnd_count_hbm, bnd_count),
        load(near_cols_hbm, near_cols),
    ]
    ld_field = [load(vol_rhs.at[:, b * BS : (b + 1) * BS], field.at[b]) for b in range(nblk)]
    ld_rhs4 = [load(vol_rhs.at[:, b * BS : (b + 1) * BS], rhs4.at[b]) for b in range(slots)]
    ld_blocks = load(vol_blocks.at[0:slots], blocks.at[0:slots])
    ld_couple = load(coupling, couple)
    ld_v = load(far_v.at[0, 0], v_mat)
    ld_u = load(far_u.at[0], u_mat)
    ld_near = load(near_blocks.at[:, 0], near)
    ld_rest = load(vol_blocks.at[slots:nblk], blocks.at[slots:nblk])

    ld_rhs_surf.wait()
    ld_inverse.wait()
    surface[...] = dot_nt(rhs_surf[...], inverse[...])

    sends = []

    def send(src, dst, ssem, rsem, device):
        copy = pltpu.make_async_remote_copy(
            src_ref=src, dst_ref=dst, send_sem=ssem, recv_sem=rsem, device_id=device,
            device_id_type=MESH,
        )
        copy.start()
        sends.append(copy)

    def arrived(dst, rsem, ssem):
        pltpu.make_async_remote_copy(
            src_ref=dst, dst_ref=dst, send_sem=ssem, recv_sem=rsem,
            device_id={"row": partner}, device_id_type=MESH,
        ).wait_recv()

    z_far_first = [k for d in range(nz // 2, 0, -1) for k in sorted({d, nz - d})]
    z_near_first = z_far_first[::-1]
    y_order = sorted(range(1, ny), key=lambda o: abs(o - ny / 2))

    def route(oz, oy):
        return CORNER[min(oz, nz - oz), min(oy, ny - oy)]

    def share(ref, way, path):
        if way == "AB":
            return ref.at[0:half] if path == "A" else ref.at[half:angles]
        return ref

    def at_row(oy):
        return y_peer(oy) * CORES + core

    z_own_order = z_near_first if NEAR_FIRST else z_far_first

    def gather_start(it):
        own = gat[it].at[core, z, y]
        own[...] = surface[...].astype(BF16)
        if it == 0:
            pl.semaphore_wait(barrier, (nz - 1) + (ny - 1) + 1 + (ncol - 1))
        for o in y_order:
            send(own, own, yo_send.at[it, o], yo_recv.at[it, y], {"row": at_row(o)})
        for o in z_own_order:
            send(own, own, zo_send.at[it, o], zo_recv.at[it, z], {"vol": z_peer(o)})
        send(own, own, co_send.at[it, 0, 0], co_recv.at[it, z, y], {"row": partner})
        for oz in z_far_first:
            for oy in y_order:
                if route(oz, oy) == "D":
                    send(
                        own, own, af_send.at[it, oz, oy], af_recv.at[it, z, y],
                        {"vol": z_peer(oz), "row": at_row(oy)},
                    )

    def from_z(it, oz):
        src = z_peer(oz)
        ref = gat[it].at[core, src, y]
        arrived(ref, zo_recv.at[it, src], zo_send.at[it, oz])
        for oy in y_order:
            if "A" in route(oz, oy):
                part = share(ref, route(oz, oy), "A")
                send(
                    part, part, af_send.at[it, oz, oy], af_recv.at[it, src, y],
                    {"row": at_row(oy)},
                )
        send(ref, ref, co_send.at[it, oz, 0], co_recv.at[it, src, y], {"row": partner})

    def from_y(it, oy):
        src = y_peer(oy)
        ref = gat[it].at[core, z, src]
        arrived(ref, yo_recv.at[it, src], yo_send.at[it, oy])
        for oz in z_far_first:
            if "B" in route(oz, oy):
                part = share(ref, route(oz, oy), "B")
                send(
                    part, part, bf_send.at[it, oz, oy], bf_recv.at[it, z, src],
                    {"vol": z_peer(oz)},
                )
        send(ref, ref, co_send.at[it, 0, oy], co_recv.at[it, z, src], {"row": partner})

    def from_both(it, oz, oy):
        z_src, y_src = z_peer(oz), y_peer(oy)
        ref = gat[it].at[core, z_src, y_src]
        way = route(oz, oy)
        if way != "B":
            arrived(share(ref, way, "A"), af_recv.at[it, z_src, y_src], af_send.at[it, oz, oy])
        if "B" in way:
            arrived(share(ref, way, "B"), bf_recv.at[it, z_src, y_src], bf_send.at[it, oz, oy])
        send(ref, ref, co_send.at[it, oz, oy], co_recv.at[it, z_src, y_src], {"row": partner})

    def far_part(it, k, oz):
        v = z_peer(oz)
        lhs, rhs = [], []
        for j in range(ny):
            lhs.append(gat[it][k, v, j])
            start = pl.multiple_of((v * ny * CORES + j * CORES + k) * BS, BS)
            rhs.append(v_mat[:, pl.ds(start, BS)])
        return dot_nt(jnp.concatenate(lhs, axis=1), jnp.concatenate(rhs, axis=1))

    def gather_finish(it):
        legs = [(d, 1, o) for o in z_near_first for d in [2 * min(o, nz - o)]]
        legs += [(3, 0, o) for o in y_order]
        for _, along_z, o in sorted(legs):
            if along_z:
                from_z(it, o)
            else:
                from_y(it, o)
        for oz in z_near_first:
            for oy in y_order:
                from_both(it, oz, oy)
        if it == 0:
            ld_v.wait()
        total = None
        for oz in [0] + z_near_first:
            term = far_part(it, core, oz)
            total = term if total is None else total + term
        for oz in [0] + z_near_first:
            v = z_peer(oz)
            for oy in [0] + y_order:
                j = y_peer(oy)
                arrived(gat[it].at[1 - core, v, j], co_recv.at[it, v, j], co_send.at[it, oz, oy])
            total += far_part(it, 1 - core, oz)
        return total.astype(BF16)

    def volume_block(b):
        lhs = jnp.concatenate([field[vol_cols[n, b]] for n in range(nnz)], axis=1)
        rhs = jnp.concatenate([blocks[b, n] for n in range(nnz)], axis=1)
        return dot_nt(lhs, rhs)

    def alive(j):
        return jnp.where(j < bnd_count[0], 1.0, 0.0).astype(F32)

    def traces(it):
        parts = []
        for j in range(slots):
            x_half = volume_block(j).astype(BF16)
            parts.append(dot_nn(x_half, couple[j]) * alive(j))
        for m in range(nz):
            total = None
            for j in range(slots):
                term = parts[j] * jnp.where(trace_map[j] == m, 1.0, 0.0).astype(F32)
                total = term if total is None else total + term
            tr_send[it, m] = total.astype(BF16)

    def traces_send(it):
        for o in [k for d in range(nz // 2, 0, -1) for k in sorted({d, nz - d})]:
            dst = z_peer(o)
            send(
                tr_send.at[it, dst], tr_recv.at[it, z], tr_ssem.at[it, o], tr_rsem.at[it, z],
                {"vol": dst},
            )

    def integral_block(it, coeffs, b):
        start = pl.multiple_of(b * BS, BS)
        lhs, rhs = [], []
        for n in range(nears):
            index = near_cols[n, b]
            v, rest = index // (ny * CORES), index % (ny * CORES)
            lhs.append(gat[it][rest % CORES, v, rest // CORES])
            rhs.append(near[b, n])
        total = dot_nt(jnp.concatenate(lhs, axis=1), jnp.concatenate(rhs, axis=1))
        return total + dot_nn(coeffs, u_mat[:, pl.ds(start, BS)])

    col_order = sorted(
        range(1, ncol), key=lambda o: (-(o % Y_HALVES), abs(o // Y_HALVES - nx / 2))
    )

    def integral_send(it, coeffs):
        for o in col_order:
            dst = col_peer(o)
            row_send[it, dst] = integral_block(it, coeffs, dst).astype(BF16)
            send(
                row_send.at[it, dst], row_recv.at[it, col], row_ssem.at[it, o],
                row_rsem.at[it, col], {"col": dst},
            )
        row_own[...] = integral_block(it, coeffs, col)

    def residual(it):
        for j in range(slots):
            index = trace_map[j]
            current = dot_nt(gat[it][core, index, y], couple[j]) * alive(j)
            field[j] = (rhs4[j].astype(F32) - current).astype(BF16)

    def surface_step(it):
        total = row_own[...] + tr_send[it, z].astype(F32)
        for o in range(1, nz):
            src = z_peer(o)
            arrived(tr_recv.at[it, src], tr_rsem.at[it, src], tr_ssem.at[it, o])
            total += tr_recv[it, src].astype(F32)
        for o in range(1, ncol):
            src = col_peer(o)
            arrived(row_recv.at[it, src], row_rsem.at[it, src], row_ssem.at[it, o])
            total += row_recv[it, src].astype(F32)
        resid = (rhs_surf[...].astype(F32) - total).astype(BF16)
        surface[...] += dot_nt(resid, inverse[...])

    for it in range(ITERS):
        if it == 0:
            for copy in ld_tables + ld_field + ld_rhs4:
                copy.wait()
            ld_blocks.wait()
            ld_couple.wait()
            traces(0)
        gather_start(it)
        coeffs = gather_finish(it)
        if it == 0:
            ld_u.wait()
            ld_near.wait()
        integral_send(it, coeffs)
        traces_send(it)
        residual(it)
        if it + 1 < ITERS:
            traces(it + 1)
        else:
            ld_rest.wait()
            for b in range(nblk):
                vol_out[:, b * BS : (b + 1) * BS] = volume_block(b)
        surface_step(it)
    surf_out[...] = surface[...]
    for copy in sends:
        copy.wait_send()


def in_hbm(x):
    if x.size == 1:
        return x
    return pltpu.with_memory_space_constraint(x, pltpu.HBM)


def local(
    sizes,
    vol_rhs,
    surf_rhs,
    vol_blocks,
    vol_cols,
    coupling,
    trace_map,
    bnd_count,
    surf_inverse,
    near_blocks,
    near_cols,
    far_u,
    far_v,
):
    nz, ny, nx = sizes
    ncol = nx * Y_HALVES
    angles = vol_rhs.shape[0]
    nblk, nnz = vol_cols.shape
    slots = coupling.shape[0]
    rank = far_u.shape[1]
    nears = near_blocks.shape[2]
    hbm = pl.BlockSpec(memory_space=pltpu.HBM)
    dma = pltpu.SemaphoreType.DMA
    return pl.pallas_call(
        functools.partial(kernel, sizes),
        out_shape=(
            jax.ShapeDtypeStruct((angles, nblk * BS), F32),
            jax.ShapeDtypeStruct((angles, BS), F32),
        ),
        in_specs=[hbm] * 2 + [pl.BlockSpec(memory_space=pl.ANY)] + [hbm] * 9,
        out_specs=(pl.BlockSpec(memory_space=pltpu.VMEM),) * 2,
        scratch_shapes=[
            pltpu.SMEM((nnz, nblk), jnp.int32),
            pltpu.SMEM((slots,), jnp.int32),
            pltpu.SMEM((1,), jnp.int32),
            pltpu.SMEM((nears, ncol), jnp.int32),
            pltpu.VMEM((slots, angles, BS), BF16),
            pltpu.VMEM((nblk, angles, BS), BF16),
            pltpu.VMEM((angles, BS), BF16),
            pltpu.VMEM((nblk, nnz, BS, BS), BF16),
            pltpu.VMEM((slots, BS, BS), BF16),
            pltpu.VMEM((BS, BS), BF16),
            pltpu.VMEM((ncol, nears, BS, BS), BF16),
            pltpu.VMEM((rank, ncol * BS), BF16),
            pltpu.VMEM((rank, nz * ny * CORES * BS), BF16),
            pltpu.VMEM((CORES, nz, ny, angles, BS), BF16),
            pltpu.VMEM((CORES, nz, ny, angles, BS), BF16),
            pltpu.VMEM((ITERS, nz, angles, BS), BF16),
            pltpu.VMEM((ITERS, nz, angles, BS), BF16),
            pltpu.VMEM((ITERS, ncol, angles, BS), BF16),
            pltpu.VMEM((ITERS, ncol, angles, BS), BF16),
            pltpu.VMEM((angles, BS), F32),
            pltpu.VMEM((angles, BS), F32),
            dma((nblk + slots + 12,)),
            dma((ITERS, nz)),
            dma((ITERS, nz)),
            dma((ITERS, ny)),
            dma((ITERS, ny)),
            dma((ITERS, nz, ny)),
            dma((ITERS, nz, ny)),
            dma((ITERS, nz, ny)),
            dma((ITERS, nz, ny)),
            dma((ITERS, nz, ny)),
            dma((ITERS, nz, ny)),
            dma((ITERS, nz)),
            dma((ITERS, nz)),
            dma((ITERS, ncol)),
            dma((ITERS, ncol)),
        ],
        compiler_params=pltpu.CompilerParams(
            collective_id=0, has_side_effects=True, vmem_limit_bytes=16 * 2**20
        ),
    )(*map(
        in_hbm, (vol_cols.T,
        trace_map,
        bnd_count,
        near_cols[:, 0].T,
        vol_rhs,
        surf_rhs,
        vol_blocks,
        coupling,
        surf_inverse,
        near_blocks,
        far_u,
        far_v,
    )))


def solution(mesh):
    sizes = (mesh.shape["vol"], mesh.shape["row"] // CORES, mesh.shape["col"] // Y_HALVES)
    everywhere = ("vol", "row", "col")
    in_specs = (
        P(None, everywhere),
        P(None, everywhere),
        P(everywhere, None, None, None),
        P(everywhere, None),
        P(everywhere, None, None),
        P(everywhere),
        P(everywhere),
        P(everywhere, None, None),
        P(("vol", "row"), "col", None, None, None),
        P(("vol", "row"), "col", None),
        P("col", None, ("vol", "row")),
        P(("vol", "row"), "col", None, None),
    )
    out_specs = (P(None, everywhere), P(None, everywhere))
    return jax.shard_map(
        functools.partial(local, sizes), mesh=mesh, in_specs=in_specs, out_specs=out_specs,
        check_vma=False,
    )
```

```python
import functools

import jax
import jax.numpy as jnp
from jax import lax
from jax.experimental import pallas as pl
from jax.experimental.pallas import tpu as pltpu
from jax.sharding import PartitionSpec as P

BS = 128
ITERS = 2
CORES = 2
Y_HALVES = 2
MESH = pl.DeviceIdType.MESH
CORNER = {(1, 1): 'AB', (1, 2): 'AB', (2, 1): 'AB', (2, 2): 'AB', (3, 1): 'AB', (3, 2): 'AB', (4, 1): 'AB', (4, 2): 'AB'}
NEAR_FIRST = True
F32 = jnp.float32
BF16 = jnp.bfloat16


def dot_nt(a, b):
    return lax.dot_general(a, b, (((1,), (1,)), ((), ())), preferred_element_type=F32)


def dot_nn(a, b):
    return lax.dot_general(a, b, (((1,), (0,)), ((), ())), preferred_element_type=F32)


def kernel(
    sizes,
    vol_cols_hbm,
    trace_map_hbm,
    bnd_count_hbm,
    near_cols_hbm,
    vol_rhs,
    surf_rhs,
    vol_blocks,
    coupling,
    surf_inverse,
    near_blocks,
    far_u,
    far_v,
    vol_out,
    surf_out,
    vol_cols,
    trace_map,
    bnd_count,
    near_cols,
    rhs4,
    field,
    rhs_surf,
    blocks,
    couple,
    inverse,
    near,
    u_mat,
    v_mat,
    gat0,
    gat1,
    tr_send,
    tr_recv,
    row_send,
    row_recv,
    row_own,
    surface,
    load_sem,
    zo_send,
    zo_recv,
    yo_send,
    yo_recv,
    af_send,
    af_recv,
    bf_send,
    bf_recv,
    co_send,
    co_recv,
    tr_ssem,
    tr_rsem,
    row_ssem,
    row_rsem,
):
    gat = (gat0, gat1)
    nz, ny, nx = sizes
    ncol = nx * Y_HALVES
    angles = rhs_surf.shape[0]
    half = angles // 2
    nblk = field.shape[0]
    nnz = blocks.shape[1]
    slots = couple.shape[0]
    nears = near.shape[1]

    z = lax.axis_index("vol")
    row = lax.axis_index("row")
    col = lax.axis_index("col")
    y, core = row // CORES, row % CORES
    x, y_hi = col // Y_HALVES, col % Y_HALVES

    def z_peer(o):
        return lax.rem(z + o, nz)

    def y_peer(o):
        return lax.rem(y + o, ny)

    def col_peer(o):
        return lax.rem(x + o // Y_HALVES, nx) * Y_HALVES + lax.rem(y_hi + o % Y_HALVES, Y_HALVES)

    partner = y * CORES + (1 - core)

    loads = []

    def load(src, dst):
        copy = pltpu.make_async_copy(src, dst, load_sem.at[len(loads)])
        copy.start()
        loads.append(copy)
        return copy

    ld_rhs_surf = load(surf_rhs, rhs_surf)
    ld_inverse = load(surf_inverse.at[0], inverse)

    barrier = pltpu.get_barrier_semaphore()
    for o in range(1, nz):
        pl.semaphore_signal(barrier, inc=1, device_id={"vol": z_peer(o)}, device_id_type=MESH)
    for o in range(1, ny):
        pl.semaphore_signal(
            barrier, inc=1, device_id={"row": y_peer(o) * CORES + core}, device_id_type=MESH
        )
    pl.semaphore_signal(barrier, inc=1, device_id={"row": partner}, device_id_type=MESH)
    for o in range(1, ncol):
        pl.semaphore_signal(barrier, inc=1, device_id={"col": col_peer(o)}, device_id_type=MESH)

    ld_tables = [
        load(vol_cols_hbm, vol_cols),
        load(trace_map_hbm, trace_map),
        load(bnd_count_hbm, bnd_count),
        load(near_cols_hbm, near_cols),
    ]
    ld_field = [load(vol_rhs.at[:, b * BS : (b + 1) * BS], field.at[b]) for b in range(nblk)]
    ld_rhs4 = [load(vol_rhs.at[:, b * BS : (b + 1) * BS], rhs4.at[b]) for b in range(slots)]
    ld_blocks = load(vol_blocks.at[0:slots], blocks.at[0:slots])
    ld_couple = load(coupling, couple)
    ld_v = load(far_v.at[0, 0], v_mat)
    ld_u = load(far_u.at[0], u_mat)
    ld_near = load(near_blocks.at[:, 0], near)
    ld_rest = load(vol_blocks.at[slots:nblk], blocks.at[slots:nblk])

    ld_rhs_surf.wait()
    ld_inverse.wait()
    surface[...] = dot_nt(rhs_surf[...], inverse[...])

    sends = []

    def send(src, dst, ssem, rsem, device):
        copy = pltpu.make_async_remote_copy(
            src_ref=src, dst_ref=dst, send_sem=ssem, recv_sem=rsem, device_id=device,
            device_id_type=MESH,
        )
        copy.start()
        sends.append(copy)

    def arrived(dst, rsem, ssem):
        pltpu.make_async_remote_copy(
            src_ref=dst, dst_ref=dst, send_sem=ssem, recv_sem=rsem,
            device_id={"row": partner}, device_id_type=MESH,
        ).wait_recv()

    z_far_first = [k for d in range(nz // 2, 0, -1) for k in sorted({d, nz - d})]
    z_near_first = z_far_first[::-1]
    y_order = sorted(range(1, ny), key=lambda o: abs(o - ny / 2))

    def route(oz, oy):
        return CORNER[min(oz, nz - oz), min(oy, ny - oy)]

    def share(ref, way, path):
        if way == "AB":
            return ref.at[0:half] if path == "A" else ref.at[half:angles]
        return ref

    def at_row(oy):
        return y_peer(oy) * CORES + core

    z_own_order = z_near_first if NEAR_FIRST else z_far_first

    def gather_start(it):
        own = gat[it].at[core, z, y]
        own[...] = surface[...].astype(BF16)
        if it == 0:
            pl.semaphore_wait(barrier, (nz - 1) + (ny - 1) + 1 + (ncol - 1))
        for o in y_order:
            send(own, own, yo_send.at[it, o], yo_recv.at[it, y], {"row": at_row(o)})
        for o in z_own_order:
            send(own, own, zo_send.at[it, o], zo_recv.at[it, z], {"vol": z_peer(o)})
        send(own, own, co_send.at[it, 0, 0], co_recv.at[it, z, y], {"row": partner})
        for oz in z_far_first:
            for oy in y_order:
                if route(oz, oy) == "D":
                    send(
                        own, own, af_send.at[it, oz, oy], af_recv.at[it, z, y],
                        {"vol": z_peer(oz), "row": at_row(oy)},
                    )

    def from_z(it, oz):
        src = z_peer(oz)
        ref = gat[it].at[core, src, y]
        arrived(ref, zo_recv.at[it, src], zo_send.at[it, oz])
        for oy in y_order:
            if "A" in route(oz, oy):
                part = share(ref, route(oz, oy), "A")
                send(
                    part, part, af_send.at[it, oz, oy], af_recv.at[it, src, y],
                    {"row": at_row(oy)},
                )
        send(ref, ref, co_send.at[it, oz, 0], co_recv.at[it, src, y], {"row": partner})

    def from_y(it, oy):
        src = y_peer(oy)
        ref = gat[it].at[core, z, src]
        arrived(ref, yo_recv.at[it, src], yo_send.at[it, oy])
        for oz in z_far_first:
            if "B" in route(oz, oy):
                part = share(ref, route(oz, oy), "B")
                send(
                    part, part, bf_send.at[it, oz, oy], bf_recv.at[it, z, src],
                    {"vol": z_peer(oz)},
                )
        send(ref, ref, co_send.at[it, 0, oy], co_recv.at[it, z, src], {"row": partner})

    def from_both(it, oz, oy):
        z_src, y_src = z_peer(oz), y_peer(oy)
        ref = gat[it].at[core, z_src, y_src]
        way = route(oz, oy)
        if way != "B":
            arrived(share(ref, way, "A"), af_recv.at[it, z_src, y_src], af_send.at[it, oz, oy])
        if "B" in way:
            arrived(share(ref, way, "B"), bf_recv.at[it, z_src, y_src], bf_send.at[it, oz, oy])
        send(ref, ref, co_send.at[it, oz, oy], co_recv.at[it, z_src, y_src], {"row": partner})

    def far_part(it, k, oz):
        v = z_peer(oz)
        lhs, rhs = [], []
        for j in range(ny):
            lhs.append(gat[it][k, v, j])
            start = pl.multiple_of((v * ny * CORES + j * CORES + k) * BS, BS)
            rhs.append(v_mat[:, pl.ds(start, BS)])
        return dot_nt(jnp.concatenate(lhs, axis=1), jnp.concatenate(rhs, axis=1))

    def gather_finish(it):
        legs = [(d, 1, o) for o in z_near_first for d in [2 * min(o, nz - o)]]
        legs += [(3, 0, o) for o in y_order]
        for _, along_z, o in sorted(legs):
            if along_z:
                from_z(it, o)
            else:
                from_y(it, o)
        for oz in z_near_first:
            for oy in y_order:
                from_both(it, oz, oy)
        if it == 0:
            ld_v.wait()
        total = None
        for oz in [0] + z_near_first:
            term = far_part(it, core, oz)
            total = term if total is None else total + term
        for oz in [0] + z_near_first:
            v = z_peer(oz)
            for oy in [0] + y_order:
                j = y_peer(oy)
                arrived(gat[it].at[1 - core, v, j], co_recv.at[it, v, j], co_send.at[it, oz, oy])
            total += far_part(it, 1 - core, oz)
        return total.astype(BF16)

    def volume_block(b):
        lhs = jnp.concatenate([field[vol_cols[n, b]] for n in range(nnz)], axis=1)
        rhs = jnp.concatenate([blocks[b, n] for n in range(nnz)], axis=1)
        return dot_nt(lhs, rhs)

    def alive(j):
        return jnp.where(j < bnd_count[0], 1.0, 0.0).astype(F32)

    def traces(it):
        parts = []
        for j in range(slots):
            x_half = volume_block(j).astype(BF16)
            parts.append(dot_nn(x_half, couple[j]) * alive(j))
        for m in range(nz):
            total = None
            for j in range(slots):
                term = parts[j] * jnp.where(trace_map[j] == m, 1.0, 0.0).astype(F32)
                total = term if total is None else total + term
            tr_send[it, m] = total.astype(BF16)

    def traces_send(it):
        for o in [k for d in range(nz // 2, 0, -1) for k in sorted({d, nz - d})]:
            dst = z_peer(o)
            send(
                tr_send.at[it, dst], tr_recv.at[it, z], tr_ssem.at[it, o], tr_rsem.at[it, z],
                {"vol": dst},
            )

    def integral_block(it, coeffs, b):
        start = pl.multiple_of(b * BS, BS)
        lhs, rhs = [], []
        for n in range(nears):
            index = near_cols[n, b]
            v, rest = index // (ny * CORES), index % (ny * CORES)
            lhs.append(gat[it][rest % CORES, v, rest // CORES])
            rhs.append(near[b, n])
        total = dot_nt(jnp.concatenate(lhs, axis=1), jnp.concatenate(rhs, axis=1))
        return total + dot_nn(coeffs, u_mat[:, pl.ds(start, BS)])

    col_order = sorted(
        range(1, ncol), key=lambda o: (-(o % Y_HALVES), abs(o // Y_HALVES - nx / 2))
    )

    def integral_send(it, coeffs):
        for o in col_order:
            dst = col_peer(o)
            row_send[it, dst] = integral_block(it, coeffs, dst).astype(BF16)
            send(
                row_send.at[it, dst], row_recv.at[it, col], row_ssem.at[it, o],
                row_rsem.at[it, col], {"col": dst},
            )
        row_own[...] = integral_block(it, coeffs, col)

    def residual(it):
        for j in range(slots):
            index = trace_map[j]
            current = dot_nt(gat[it][core, index, y], couple[j]) * alive(j)
            field[j] = (rhs4[j].astype(F32) - current).astype(BF16)

    def surface_step(it):
        total = row_own[...] + tr_send[it, z].astype(F32)
        for o in range(1, nz):
            src = z_peer(o)
            arrived(tr_recv.at[it, src], tr_rsem.at[it, src], tr_ssem.at[it, o])
            total += tr_recv[it, src].astype(F32)
        for o in range(1, ncol):
            src = col_peer(o)
            arrived(row_recv.at[it, src], row_rsem.at[it, src], row_ssem.at[it, o])
            total += row_recv[it, src].astype(F32)
        resid = (rhs_surf[...].astype(F32) - total).astype(BF16)
        surface[...] += dot_nt(resid, inverse[...])

    for it in range(ITERS):
        if it == 0:
            for copy in ld_tables + ld_field + ld_rhs4:
                copy.wait()
            ld_blocks.wait()
            ld_couple.wait()
            traces(0)
        gather_start(it)
        coeffs = gather_finish(it)
        early = len(sends)
        if it == 0:
            ld_u.wait()
            ld_near.wait()
        integral_send(it, coeffs)
        traces_send(it)
        residual(it)
        if it + 1 < ITERS:
            traces(it + 1)
        else:
            ld_rest.wait()
            for b in range(nblk):
                vol_out[:, b * BS : (b + 1) * BS] = volume_block(b)
        if it + 1 == ITERS:
            for copy in sends[:early]:
                copy.wait_send()
        surface_step(it)
    surf_out[...] = surface[...]
    for copy in sends[early:]:
        copy.wait_send()


def in_hbm(x):
    if x.size == 1:
        return x
    return pltpu.with_memory_space_constraint(x, pltpu.HBM)


def local(
    sizes,
    vol_rhs,
    surf_rhs,
    vol_blocks,
    vol_cols,
    coupling,
    trace_map,
    bnd_count,
    surf_inverse,
    near_blocks,
    near_cols,
    far_u,
    far_v,
):
    nz, ny, nx = sizes
    ncol = nx * Y_HALVES
    angles = vol_rhs.shape[0]
    nblk, nnz = vol_cols.shape
    slots = coupling.shape[0]
    rank = far_u.shape[1]
    nears = near_blocks.shape[2]
    hbm = pl.BlockSpec(memory_space=pltpu.HBM)
    dma = pltpu.SemaphoreType.DMA
    return pl.pallas_call(
        functools.partial(kernel, sizes),
        out_shape=(
            jax.ShapeDtypeStruct((angles, nblk * BS), F32),
            jax.ShapeDtypeStruct((angles, BS), F32),
        ),
        in_specs=[hbm] * 2 + [pl.BlockSpec(memory_space=pl.ANY)] + [hbm] * 9,
        out_specs=(pl.BlockSpec(memory_space=pltpu.VMEM),) * 2,
        scratch_shapes=[
            pltpu.SMEM((nnz, nblk), jnp.int32),
            pltpu.SMEM((slots,), jnp.int32),
            pltpu.SMEM((1,), jnp.int32),
            pltpu.SMEM((nears, ncol), jnp.int32),
            pltpu.VMEM((slots, angles, BS), BF16),
            pltpu.VMEM((nblk, angles, BS), BF16),
            pltpu.VMEM((angles, BS), BF16),
            pltpu.VMEM((nblk, nnz, BS, BS), BF16),
            pltpu.VMEM((slots, BS, BS), BF16),
            pltpu.VMEM((BS, BS), BF16),
            pltpu.VMEM((ncol, nears, BS, BS), BF16),
            pltpu.VMEM((rank, ncol * BS), BF16),
            pltpu.VMEM((rank, nz * ny * CORES * BS), BF16),
            pltpu.VMEM((CORES, nz, ny, angles, BS), BF16),
            pltpu.VMEM((CORES, nz, ny, angles, BS), BF16),
            pltpu.VMEM((ITERS, nz, angles, BS), BF16),
            pltpu.VMEM((ITERS, nz, angles, BS), BF16),
            pltpu.VMEM((ITERS, ncol, angles, BS), BF16),
            pltpu.VMEM((ITERS, ncol, angles, BS), BF16),
            pltpu.VMEM((angles, BS), F32),
            pltpu.VMEM((angles, BS), F32),
            dma((nblk + slots + 12,)),
            dma((ITERS, nz)),
            dma((ITERS, nz)),
            dma((ITERS, ny)),
            dma((ITERS, ny)),
            dma((ITERS, nz, ny)),
            dma((ITERS, nz, ny)),
            dma((ITERS, nz, ny)),
            dma((ITERS, nz, ny)),
            dma((ITERS, nz, ny)),
            dma((ITERS, nz, ny)),
            dma((ITERS, nz)),
            dma((ITERS, nz)),
            dma((ITERS, ncol)),
            dma((ITERS, ncol)),
        ],
        compiler_params=pltpu.CompilerParams(
            collective_id=0, has_side_effects=True, vmem_limit_bytes=16 * 2**20
        ),
    )(*map(
        in_hbm, (vol_cols.T,
        trace_map,
        bnd_count,
        near_cols[:, 0].T,
        vol_rhs,
        surf_rhs,
        vol_blocks,
        coupling,
        surf_inverse,
        near_blocks,
        far_u,
        far_v,
    )))


def solution(mesh):
    sizes = (mesh.shape["vol"], mesh.shape["row"] // CORES, mesh.shape["col"] // Y_HALVES)
    everywhere = ("vol", "row", "col")
    in_specs = (
        P(None, everywhere),
        P(None, everywhere),
        P(everywhere, None, None, None),
        P(everywhere, None),
        P(everywhere, None, None),
        P(everywhere),
        P(everywhere),
        P(everywhere, None, None),
        P(("vol", "row"), "col", None, None, None),
        P(("vol", "row"), "col", None),
        P("col", None, ("vol", "row")),
        P(("vol", "row"), "col", None, None),
    )
    out_specs = (P(None, everywhere), P(None, everywhere))
    return jax.shard_map(
        functools.partial(local, sizes), mesh=mesh, in_specs=in_specs, out_specs=out_specs,
        check_vma=False,
    )
```
